32 devices in a mesh: groups: 2 (over x), wide: 16 (over z, y, core).
Axes of the slice: x: 2, y: 2, z: 4, core: 2. Of those that a mesh axis runs over, the one named last changes fastest.
Arguments:
- queries: bfloat16 [32, 12, 8192], P(('groups', 'wide')), parts along dimension 0, may hold values from -4.5 to 4.5
- prefix_kv: bfloat16 [32, 2, 1024, 1024], P(('groups', 'wide')), parts along dimension 0, may hold values from -4.5 to 4.5
- suffix_kv: bfloat16 [32, 12, 2, 64, 1024], P(('groups', 'wide')), parts along dimension 0, may hold values from -4.5 to 4.5
- counts: int32 [32], P('groups'), parts along dimension 0, may hold values from 1 to 12, 128 in all
- residual: bfloat16 [384, 8192], P('groups', 'wide'), parts along dimension 0, may hold values from -16 to 16
- out_weight: bfloat16 [8192, 8192], P(None, 'wide'), may hold values from -0.5 to 0.5
- norm_gain: float32 [8192], replicated, may hold values from 0.1 to 1.9
- qkv_weight: bfloat16 [8192, 10240], P(None, 'wide'), may hold values from -0.0625 to 0.0625
- owners: int32 [16, 8], replicated, may hold values from 0 to 15, as said below
Outputs:
- regrouped: bfloat16 [32, 2, 12, 8, 1280], P(('groups', 'wide')), parts along dimension 0
The draws below stay inside these ranges and needn't reach their ends.
There are 2 independent parts, one for each index of `groups`. The reference program is written for one: setup_inputs(seed, part) draws one part's arguments, and reference() takes and returns one part's arrays. A program takes and returns all parts, laid end to end along the dimension named above; an argument that names none is the same for every part. Nothing has to cross between parts.
Inputs may be any that keep to these rules, and one draw needn't show every extreme that they name: counts[p] rows of parent p are live, in slots 0 to counts[p] - 1; they sum to 128 and the largest is 12. `owners`: within each key-value group every device owns at most 2 parents; in every group some devices own exactly 2 and some none.
All inputs are finite; a program needn't handle non-finite values.
Results may differ from the reference program's by a relative error of at most 0.012.
Values may be sent and summed in bfloat16 or wider, within the bound.
No kernel may reach another device: no remote copies, remote signals or barrier semaphores. Data moves between devices by JAX's collectives and lax.ppermute only.
A program may use at most 128 MiB of HBM per device.

```python
import math
import jax
import jax.numpy as jnp
import numpy as np
from jax import lax

KVH = 8
HD = 128
D = 8192
GQ = 8
GCOLS = 1280
QCOLS = 10240
CTX = 1024
SUF = 64
CAP = 12
OWN_G = 2
PARENTS = 16
ROWS = 128
SLOTS = 192
N_WIDE = 16


def draw_queries(key, part):
    noise_key = jax.random.fold_in(key, 1)
    shape_full = (PARENTS, CAP, KVH, GQ, HD)
    values = jnp.clip(1.5 * jax.random.normal(noise_key, shape_full, jnp.float32), -4.5, 4.5)
    return values.reshape(PARENTS, CAP, D).astype(jnp.bfloat16)


def draw_prefix_kv(key, part):
    noise_key = jax.random.fold_in(key, 2)
    shape_full = (PARENTS, 2, CTX, KVH, HD)
    values = jnp.clip(jax.random.normal(noise_key, shape_full, jnp.float32), -4.5, 4.5)
    return values.reshape(PARENTS, 2, CTX, KVH * HD).astype(jnp.bfloat16)


def draw_residual(key, part):
    sample_key = jax.random.fold_in(key, 5)
    column_key, row_key, noise_key = jax.random.split(sample_key, 3)
    columns = jnp.arange(D).astype(jnp.float32) / D
    column_scale = 3.0 ** columns * jnp.exp(jax.random.uniform(column_key, (D,), jnp.float32) * jnp.log(3.4)) / 2.2
    row_scale = jnp.exp(jax.random.uniform(row_key, (SLOTS, 1), jnp.float32) * jnp.log(10.0)) / 3.0
    values = jax.random.normal(noise_key, (SLOTS, D), jnp.float32)
    return jnp.clip(values * row_scale * column_scale, -16.0, 16.0).astype(jnp.bfloat16)


def draw_owners(key, part):
    quarter = PARENTS // 4
    owner_columns = []
    for kv_group in range(KVH):
        group_key = jax.random.fold_in(key, 17 + kv_group)
        device_key, order_key = jax.random.split(group_key)
        device_order = jax.random.permutation(device_key, PARENTS)
        slot_list = jnp.concatenate([jnp.repeat(device_order[:quarter], 2), device_order[2 * quarter:]])
        parent_order = jax.random.permutation(order_key, PARENTS)
        owner_columns.append(jnp.zeros((PARENTS,), jnp.int32).at[parent_order].set(slot_list.astype(jnp.int32)))
    return jnp.stack(owner_columns, axis=1).astype(jnp.int32)


def block_levels(key, extent, pieces, low, high):
    level, own = 1.0, jax.random.fold_in(key, 6)
    for dim, parts in pieces:
        draws = jnp.exp(jax.random.uniform(jax.random.fold_in(own, dim), (parts,), jnp.float32, low / len(pieces), high / len(pieces)))
        level = level * jnp.repeat(draws, extent[dim] // parts).reshape([-1 if axis == dim else 1 for axis in range(len(extent))])
    return level


def split_up(amount, total, most, lean):
    portions = [(1 << 20) // math.isqrt(standing ** lean) + 1 for standing in range(2, amount + 1)]
    surplus, given = total - most - (amount - 1), [1] * (amount - 1)
    while surplus > 0:
        candidates = [i for i in range(amount - 1) if given[i] < most]
        mass, budget = sum([portions[i] for i in candidates]), surplus
        for i in candidates:
            addition = min(most - given[i], max(1, budget * portions[i] // mass), surplus)
            given[i] = given[i] + addition
            surplus = surplus - addition
    return np.array([most] + given)


def uneven_parts(rng, amount, total, limit, skew):
    if amount == 2:
        one = jax.random.randint(rng, (), max(1, total - limit), min(limit, total - 1) + 1)
        return jnp.stack([one, total - one])
    sizes = jnp.asarray(split_up(amount, total, limit, skew), jnp.int32)
    twos = (amount - 1) // 2
    donor, receiver = sizes[1:1 + 2 * twos:2], sizes[2:2 + 2 * twos:2]
    slack = jnp.minimum(donor - 1, limit - receiver)
    passed = jax.random.randint(jax.random.fold_in(rng, 1), (twos,), 0, 1 << 20) % (slack + 1)
    sizes = sizes.at[1:1 + 2 * twos:2].set(donor - passed).at[2:2 + 2 * twos:2].set(receiver + passed)
    return sizes[jax.random.permutation(jax.random.fold_in(rng, 2), amount)]


def scatter_about(rng, dims, deviation, most, cuts=(), kind=jnp.bfloat16):
    loudness = block_levels(rng, dims, cuts, -0.22, 0.18) if cuts else 1.0
    result = jax.random.normal(rng, dims, jnp.float32) * deviation * loudness
    return jnp.minimum(jnp.maximum(result, -most), most).astype(kind)


def setup_inputs(seed: int = 0, part: int = 0) -> dict:
    splits = jax.random.split(jax.random.key(seed), 10)
    part_splits = jax.random.split(jax.random.fold_in(splits[9], part), 10)
    queries = draw_queries(jax.random.fold_in(jax.random.fold_in(splits[9], part), 71), part)
    prefix_kv = draw_prefix_kv(jax.random.fold_in(jax.random.fold_in(splits[9], part), 71), part)
    suffix_kv = scatter_about(part_splits[2], (PARENTS, CAP, 2, SUF, KVH * HD), 1.0, 4.5, ((0, 16),))
    counts = uneven_parts(part_splits[3], PARENTS, ROWS, CAP, 2).astype(jnp.int32)
    residual = draw_residual(jax.random.fold_in(jax.random.fold_in(splits[9], part), 71), part)
    out_weight = scatter_about(splits[5], (D, D), (D // 64) ** -0.5, 0.5, ((1, 16),))
    norm_gain = jnp.clip(1.0 + 0.18 * jax.random.normal(splits[6], (D,), jnp.float32), 0.1, 1.9)
    qkv_weight = scatter_about(splits[7], (D, QCOLS), D ** -0.5, 0.0625, ((1, 16),))
    owners = draw_owners(jax.random.fold_in(splits[9], 71), part)
    return dict(queries=queries, prefix_kv=prefix_kv, suffix_kv=suffix_kv, counts=counts, residual=residual, out_weight=out_weight, norm_gain=norm_gain, qkv_weight=qkv_weight, owners=owners)


def reference(queries, prefix_kv, suffix_kv, counts, residual, out_weight, norm_gain, qkv_weight, owners):
    score_scale = HD ** (-0.5)
    slot_rows = jnp.arange(CAP, dtype=jnp.int32)

    def one_parent(packed):
        query_rows, prefix_block, suffix_block, live_count = packed
        query_heads = query_rows.reshape(CAP, KVH, GQ, HD).astype(jnp.float32)
        prefix_keys = prefix_block[0].reshape(CTX, KVH, HD).astype(jnp.float32)
        prefix_values = prefix_block[1].reshape(CTX, KVH, HD).astype(jnp.float32)
        suffix_keys = suffix_block[:, 0].reshape(CAP, SUF, KVH, HD).astype(jnp.float32)
        suffix_values = suffix_block[:, 1].reshape(CAP, SUF, KVH, HD).astype(jnp.float32)
        distant = jnp.einsum('rgqd,tgd->rgqt', query_heads, prefix_keys) * score_scale
        nearby = jnp.einsum('rgqd,rsgd->rgqs', query_heads, suffix_keys) * score_scale
        highest = jnp.maximum(lax.optimization_barrier(jnp.max(distant, axis=-1)), lax.optimization_barrier(jnp.max(nearby, axis=-1)))[..., None]
        distant_exp = jnp.exp(distant - highest)
        nearby_exp = jnp.exp(nearby - highest)
        denominator = lax.optimization_barrier(jnp.sum(distant_exp, axis=-1, keepdims=True)) + lax.optimization_barrier(jnp.sum(nearby_exp, axis=-1, keepdims=True))
        distant_probs = lax.optimization_barrier((distant_exp / denominator).astype(jnp.bfloat16)).astype(jnp.float32)
        nearby_probs = lax.optimization_barrier((nearby_exp / denominator).astype(jnp.bfloat16)).astype(jnp.float32)
        mixed_heads = jnp.einsum('rgqt,tgd->rgqd', distant_probs, prefix_values)
        mixed_heads = mixed_heads + jnp.einsum('rgqs,rsgd->rgqd', nearby_probs, suffix_values)
        mixed_heads = mixed_heads.astype(jnp.bfloat16)
        is_valid = (slot_rows < live_count)[:, None, None, None]
        mixed_heads = jnp.where(is_valid, mixed_heads, jnp.zeros_like(mixed_heads))
        return mixed_heads.reshape(CAP, D)
    attended = lax.map(one_parent, (queries, prefix_kv, suffix_kv, counts)).reshape(SLOTS, D)
    stream = (residual.astype(jnp.float32) + jnp.dot(attended, out_weight, preferred_element_type=jnp.float32)).astype(jnp.bfloat16)
    stream_wide = stream.astype(jnp.float32)
    inverse = lax.rsqrt(lax.optimization_barrier(jnp.mean(stream_wide * stream_wide, axis=1, keepdims=True)) + 1e-05)
    normed = (stream_wide * inverse * norm_gain[None, :]).astype(jnp.bfloat16)
    projected = jnp.dot(normed, qkv_weight, preferred_element_type=jnp.float32).astype(jnp.bfloat16)
    slot_valid = (slot_rows[None, :] < counts[:, None]).reshape(SLOTS, 1)
    projected = jnp.where(slot_valid, projected, jnp.zeros_like(projected))
    device_ids = jnp.arange(N_WIDE, dtype=jnp.int32)
    member = owners[None, :, :] == device_ids[:, None, None]
    ranking = jnp.cumsum(member.astype(jnp.int32), axis=1) - 1
    slot_ids = jnp.arange(OWN_G, dtype=jnp.int32)
    chosen = member[:, None, :, :] & (ranking[:, None, :, :] == slot_ids[None, :, None, None])
    blocks = projected.reshape(PARENTS, CAP, KVH, GCOLS).astype(jnp.float32)
    regrouped = jnp.einsum('ejpg,prgf->ejrgf', chosen.astype(jnp.float32), blocks)
    return regrouped.astype(jnp.bfloat16)
```

```python
import jax
import jax.numpy as jnp
import numpy as np
from jax import lax
from jax.sharding import PartitionSpec as P

KVH = 8
HD = 128
D = 8192
GQ = 8
GCOLS = 1280
CTX = 1024
SUF = 64
CAP = 12
OWN_G = 2
MEAN_LIVE = 8


def chip_ring(devices):
    chips = devices // 2
    if chips <= 8 and chips % 2 == 0:
        return list(range(0, chips, 2)) + list(range(chips - 1, 0, -2))
    return list(range(chips))


def ring_plan(devices):
    ring = chip_ring(devices)
    n = len(ring)
    step = {}
    for name, d in (("up", 1), ("down", -1)):
        step[name] = [
            (ring[k] * 2 + c, ring[(k + d) % n] * 2 + c) for k in range(n) for c in range(2)
        ]
    step["swap"] = [(i, i ^ 1) for i in range(devices)]
    order = np.zeros((devices, devices), np.int32)
    for k in range(n):
        for c in range(2):
            order[ring[k] * 2 + c] = [
                ring[(k + s) % n] * 2 + (c ^ t) for s in range(n) for t in range(2)
            ]
    return n, step, order


def ring_gather(block, n, step, long_up):
    pieces = [None] * n
    pieces[0] = block
    up = down = block
    up_steps = n // 2 if long_up else (n - 1) // 2
    down_steps = n - 1 - up_steps
    for s in range(1, max(up_steps, down_steps) + 1):
        if s <= up_steps:
            up = lax.ppermute(up, "wide", step["up"])
            pieces[n - s] = up
        if s <= down_steps:
            down = lax.ppermute(down, "wide", step["down"])
            pieces[s] = down
    both = []
    for piece in pieces:
        both += [piece, lax.ppermute(piece, "wide", step["swap"])]
    return both


def attention(queries, prefix_kv, suffix_kv):
    score_scale = HD ** (-0.5)
    query_heads = queries[0].reshape(CAP, KVH, GQ, HD)
    prefix_keys = prefix_kv[0, 0].reshape(CTX, KVH, HD)
    prefix_values = prefix_kv[0, 1].reshape(CTX, KVH, HD)
    suffix_keys = suffix_kv[0, :, 0].reshape(CAP, SUF, KVH, HD)
    suffix_values = suffix_kv[0, :, 1].reshape(CAP, SUF, KVH, HD)
    distant = (
        jnp.einsum("rgqd,tgd->rgqt", query_heads, prefix_keys, preferred_element_type=jnp.float32)
        * score_scale
    )
    nearby = (
        jnp.einsum("rgqd,rsgd->rgqs", query_heads, suffix_keys, preferred_element_type=jnp.float32)
        * score_scale
    )
    highest = jnp.maximum(jnp.max(distant, axis=-1), jnp.max(nearby, axis=-1))[..., None]
    distant_exp = jnp.exp(distant - highest)
    nearby_exp = jnp.exp(nearby - highest)
    denominator = jnp.sum(distant_exp, axis=-1, keepdims=True) + jnp.sum(
        nearby_exp, axis=-1, keepdims=True
    )
    distant_probs = (distant_exp / denominator).astype(jnp.bfloat16)
    nearby_probs = (nearby_exp / denominator).astype(jnp.bfloat16)
    mixed_heads = jnp.einsum(
        "rgqt,tgd->rgqd", distant_probs, prefix_values, preferred_element_type=jnp.float32
    )
    mixed_heads = mixed_heads + jnp.einsum(
        "rgqs,rsgd->rgqd", nearby_probs, suffix_values, preferred_element_type=jnp.float32
    )
    return mixed_heads.astype(jnp.bfloat16).reshape(CAP, D)


def body(
    queries, prefix_kv, suffix_kv, counts, residual, out_weight, norm_gain, qkv_weight, owners
):
    devices = lax.axis_size("wide")
    my_index = lax.axis_index("wide")
    n, step, order_table = ring_plan(devices)
    order = lax.dynamic_index_in_dim(jnp.asarray(order_table), my_index, 0, keepdims=False)
    live = devices * MEAN_LIVE
    slot_rows = jnp.arange(CAP, dtype=jnp.int32)
    live_ids = jnp.arange(live, dtype=jnp.int32)
    starts = jnp.cumsum(counts) - counts

    attended = attention(queries, prefix_kv, suffix_kv)
    gathered = jnp.concatenate(ring_gather(attended, n, step, True), axis=0)
    mixed_rows = jnp.dot(gathered, out_weight, preferred_element_type=jnp.float32)
    width = residual.shape[1]
    ordered = residual.reshape(devices, CAP, width)[order].reshape(devices * CAP, width)
    stream = (ordered.astype(jnp.float32) + mixed_rows).astype(jnp.bfloat16)
    place = jnp.where(
        slot_rows[None, :] < counts[order][:, None],
        starts[order][:, None] + slot_rows[None, :],
        -1,
    ).reshape(devices * CAP)
    pack = (live_ids[:, None] == place[None, :]).astype(jnp.bfloat16)
    packed = jnp.dot(pack, stream, preferred_element_type=jnp.float32).astype(jnp.bfloat16)

    parts = ring_gather(packed, n, step, True)
    total = jnp.zeros((live, qkv_weight.shape[1]), jnp.float32)
    squares = jnp.zeros((live, 1), jnp.float32)
    for k, part in enumerate(parts):
        first = order[k] * width
        gain = lax.dynamic_slice_in_dim(norm_gain, first, width, 0)
        weight = lax.dynamic_slice_in_dim(qkv_weight, first, width, 0)
        wide = part.astype(jnp.float32)
        squares = squares + jnp.sum(wide * wide, axis=1, keepdims=True)
        total = total + jnp.dot(
            (wide * gain[None, :]).astype(jnp.bfloat16),
            weight,
            preferred_element_type=jnp.float32,
        )
    inverse = lax.rsqrt(squares / D + 1e-05)
    projected = (total * inverse).astype(jnp.bfloat16)

    kv_group = my_index // (devices // KVH)
    column_owner = lax.dynamic_index_in_dim(owners, kv_group, 1, keepdims=False)
    device_ids = jnp.arange(devices, dtype=jnp.int32)
    member = column_owner[None, :] == device_ids[:, None]
    ranking = jnp.cumsum(member.astype(jnp.int32), axis=1) - 1
    slot_ids = jnp.arange(OWN_G, dtype=jnp.int32)
    chosen = member[None, :, :] & (ranking[None, :, :] == slot_ids[:, None, None])
    chosen = chosen.astype(jnp.int32)
    begin = jnp.sum(chosen * starts[None, None, :], axis=2)
    size = jnp.sum(chosen * counts[None, None, :], axis=2)
    source = jnp.where(
        slot_rows[None, :, None] < size[:, None, :],
        begin[:, None, :] + slot_rows[None, :, None],
        -1,
    )
    select = (source[..., None] == live_ids).astype(jnp.bfloat16)
    outgoing = jnp.einsum(
        "jret,tf->jref", select, projected, preferred_element_type=jnp.float32
    ).astype(jnp.bfloat16)
    incoming = lax.all_to_all(outgoing, "wide", split_axis=2, concat_axis=2, tiled=True)
    return incoming.reshape(1, OWN_G, CAP, KVH, GCOLS)


def solution(mesh):
    placed = (
        P(("groups", "wide"), None, None),
        P(("groups", "wide"), None, None, None),
        P(("groups", "wide"), None, None, None, None),
        P("groups"),
        P("groups", "wide"),
        P(None, "wide"),
        P(),
        P(None, "wide"),
        P(),
    )
    return jax.shard_map(
        body,
        mesh=mesh,
        in_specs=placed,
        out_specs=P(("groups", "wide"), None, None, None, None),
        check_vma=False,
    )
```

```python
import functools

import jax
import jax.numpy as jnp
import numpy as np
from jax import lax
from jax.experimental import pallas as pl
from jax.experimental.pallas import tpu as pltpu
from jax.sharding import PartitionSpec as P

KVH = 8
HD = 128
D = 8192
GQ = 8
GCOLS = 1280
CTX = 1024
SUF = 64
CAP = 12
OWN_G = 2
MEAN_LIVE = 8

HALVES = 2
HALF_G = KVH // HALVES
PAD = 16
LOG2E = 1.4426950408889634


ANY = pl.BlockSpec(memory_space=pl.ANY)
SMEM = pl.BlockSpec(memory_space=pltpu.SMEM)
VMEM = pl.BlockSpec(memory_space=pltpu.VMEM)


def chip_ring(devices):
    chips = devices // 2
    if chips <= 8 and chips % 2 == 0:
        return list(range(0, chips, 2)) + list(range(chips - 1, 0, -2))
    return list(range(chips))


def ring_plan(devices):
    ring = chip_ring(devices)
    n = len(ring)
    step = {}
    for name, d in (("up", 1), ("down", -1)):
        step[name] = [
            (ring[k] * 2 + c, ring[(k + d) % n] * 2 + c) for k in range(n) for c in range(2)
        ]
    step["swap"] = [(i, i ^ 1) for i in range(devices)]
    order = np.zeros((devices, devices), np.int32)
    for k in range(n):
        for c in range(2):
            order[ring[k] * 2 + c] = [
                ring[(k + s) % n] * 2 + (c ^ t) for s in range(n) for t in range(2)
            ]
    return n, step, order


def ring_gather(block, n, step, long_up):
    pieces = [None] * n
    pieces[0] = block
    up = down = block
    up_steps = n // 2 if long_up else (n - 1) // 2
    down_steps = n - 1 - up_steps
    arrivals = [[0]]
    for s in range(1, max(up_steps, down_steps) + 1):
        now = []
        if s <= up_steps:
            up = lax.ppermute(up, "wide", step["up"])
            pieces[n - s] = up
            now.append(n - s)
        if s <= down_steps:
            down = lax.ppermute(down, "wide", step["down"])
            pieces[s] = down
            now.append(s)
        arrivals.append(now)
    both = []
    for piece in pieces:
        both += [piece, lax.ppermute(piece, "wide", step["swap"])]
    return both, arrivals


def attend_kernel(half, q_ref, kv_hbm, suffix_hbm, out_ref, kv, suffix, heads, sems):
    copies = []
    for g in range(HALF_G):
        columns = pl.ds((half * HALF_G + g) * HD, HD)
        copies.append(
            (
                pltpu.make_async_copy(kv_hbm.at[0, :, :, columns], kv.at[g], sems.at[g, 0]),
                pltpu.make_async_copy(
                    suffix_hbm.at[0, :, :, :, columns], suffix.at[g], sems.at[g, 1]
                ),
            )
        )
        for copy in copies[-1]:
            copy.start()
    heads[...] = jnp.zeros_like(heads)
    rows = GQ * PAD
    own_row = lax.broadcasted_iota(jnp.int32, (rows, CAP * SUF), 0) % PAD
    own_key = lax.broadcasted_iota(jnp.int32, (rows, CAP * SUF), 1) // SUF
    mine = own_row == own_key
    scale = HD ** (-0.5) * LOG2E
    contract = (((1,), (1,)), ((), ()))
    for g in range(HALF_G):
        for q in range(GQ):
            col = (g * GQ + q) * HD
            heads[q * PAD : q * PAD + CAP, :] = q_ref[0, :, col : col + HD]
        for copy in copies[g]:
            copy.wait()
        query = heads[...]
        far = lax.dot_general(query, kv[g, 0], contract, preferred_element_type=jnp.float32)
        near = lax.dot_general(
            query,
            suffix[g, :, 0].reshape(CAP * SUF, HD),
            contract,
            preferred_element_type=jnp.float32,
        )
        near = jnp.where(mine, near, -1e30)
        top = jnp.maximum(
            jnp.max(far, axis=1, keepdims=True), jnp.max(near, axis=1, keepdims=True)
        )
        far = jnp.exp2((far - top) * scale)
        near = jnp.exp2((near - top) * scale)
        total = jnp.sum(far, axis=1, keepdims=True) + jnp.sum(near, axis=1, keepdims=True)
        mixed = jnp.dot(far.astype(jnp.bfloat16), kv[g, 1], preferred_element_type=jnp.float32)
        mixed = mixed + jnp.dot(
            near.astype(jnp.bfloat16),
            suffix[g, :, 1].reshape(CAP * SUF, HD),
            preferred_element_type=jnp.float32,
        )
        mixed = (mixed / total).astype(jnp.bfloat16)
        for q in range(GQ):
            out_ref[g * CAP : (g + 1) * CAP, q * HD : (q + 1) * HD] = mixed[
                q * PAD : q * PAD + CAP, :
            ]


def attend(half, queries, prefix_kv, suffix_kv):
    columns = HALF_G * GQ * HD
    keys = CTX + CAP * SUF
    return pl.pallas_call(
        functools.partial(attend_kernel, half),
        out_shape=jax.ShapeDtypeStruct((HALF_G * CAP, GQ * HD), jnp.bfloat16),
        grid=(1,),
        in_specs=[pl.BlockSpec((1, CAP, columns), lambda i: (0, 0, half)), ANY, ANY],
        out_specs=VMEM,
        scratch_shapes=[
            pltpu.VMEM((HALF_G, 2, CTX, HD), jnp.bfloat16),
            pltpu.VMEM((HALF_G, CAP, 2, SUF, HD), jnp.bfloat16),
            pltpu.VMEM((GQ * PAD, HD), jnp.bfloat16),
            pltpu.SemaphoreType.DMA((HALF_G, 2)),
        ],
        cost_estimate=pl.CostEstimate(
            flops=4 * HALF_G * GQ * PAD * keys * HD,
            bytes_accessed=4 * HALF_G * keys * HD,
            transcendentals=HALF_G * GQ * PAD * keys,
        ),
        name=f"attend_{half}",
    )(queries, prefix_kv, suffix_kv)


def mix_kernel(half, slots, *refs):
    pieces = refs[:slots]
    weight_hbm = refs[slots]
    lhs, weight, sems = refs[-3:]
    depth = GQ * HD
    copies = []
    for g in range(HALF_G):
        first = (half * HALF_G + g) * depth
        copies.append(
            pltpu.make_async_copy(
                weight_hbm.at[pl.ds(first, depth), :], weight.at[g], sems.at[g]
            )
        )
        copies[-1].start()
    total = None
    lhs[...] = jnp.zeros_like(lhs)
    for g in range(HALF_G):
        for m in range(slots):
            lhs[m * PAD : m * PAD + CAP, :] = pieces[m][g * CAP : (g + 1) * CAP, :]
        copies[g].wait()
        term = jnp.dot(lhs[...], weight[g], preferred_element_type=jnp.float32)
        total = term if total is None else total + term
    if half < HALVES - 1:
        refs[slots + 1][...] = total
        return
    before, order, counts, residual = refs[slots + 1 : slots + 5]
    outs = refs[slots + 5 : -4]
    starts = refs[-4]
    running = jnp.int32(0)
    for p in range(slots):
        starts[p] = running
        running = running + counts[p]
    rows = slots * PAD
    live = slots * MEAN_LIVE
    lane_slot = lax.broadcasted_iota(jnp.int32, (1, rows), 1) // PAD
    lane_row = lax.broadcasted_iota(jnp.int32, (1, rows), 1) % PAD
    tall_slot = lax.broadcasted_iota(jnp.int32, (rows, slots * CAP), 0) // PAD
    tall_row = lax.broadcasted_iota(jnp.int32, (rows, slots * CAP), 0) % PAD
    place = jnp.full((1, rows), -1, jnp.int32)
    wanted = jnp.full((rows, slots * CAP), -1, jnp.int32)
    for m in range(slots):
        parent = order[m]
        place = jnp.where(
            (lane_slot == m) & (lane_row < counts[parent]), starts[parent] + lane_row, place
        )
        wanted = jnp.where((tall_slot == m) & (tall_row < CAP), parent * CAP + tall_row, wanted)
    spread = wanted == lax.broadcasted_iota(jnp.int32, (rows, slots * CAP), 1)
    pack = place == lax.broadcasted_iota(jnp.int32, (live, rows), 0)
    ordered = jnp.dot(
        spread.astype(jnp.float32).astype(jnp.bfloat16),
        residual[...],
        preferred_element_type=jnp.float32,
    )
    stream = (ordered + (before[...] + total)).astype(jnp.bfloat16)
    packed = jnp.dot(
        pack.astype(jnp.float32).astype(jnp.bfloat16), stream, preferred_element_type=jnp.float32
    ).astype(jnp.bfloat16)
    width = packed.shape[1] // len(outs)
    for i, out in enumerate(outs):
        out[...] = packed[:, i * width : (i + 1) * width]


def mix(half, pieces, out_weight, extra, chunks):
    slots = len(pieces)
    width = out_weight.shape[1]
    rows = slots * PAD
    last = half == HALVES - 1
    depth = GQ * HD
    if last:
        live = slots * MEAN_LIVE
        out_shape = [jax.ShapeDtypeStruct((live, width // chunks), jnp.bfloat16)] * chunks
        extra_specs = [VMEM, SMEM, SMEM, VMEM]
        scratch = [pltpu.SMEM((slots,), jnp.int32)]
    else:
        out_shape = jax.ShapeDtypeStruct((rows, width), jnp.float32)
        extra_specs = []
        scratch = []
    return pl.pallas_call(
        functools.partial(mix_kernel, half, slots),
        out_shape=out_shape,
        in_specs=[VMEM] * slots + [ANY] + extra_specs,
        out_specs=[VMEM] * chunks if last else VMEM,
        scratch_shapes=scratch
        + [
            pltpu.VMEM((rows, depth), jnp.bfloat16),
            pltpu.VMEM((HALF_G, depth, width), jnp.bfloat16),
            pltpu.SemaphoreType.DMA((HALF_G,)),
        ],
        cost_estimate=pl.CostEstimate(
            flops=2 * rows * HALF_G * depth * width,
            bytes_accessed=2 * HALF_G * depth * (width + slots * CAP),
            transcendentals=0,
        ),
        name=f"mix_{half}",
    )(*pieces, out_weight, *extra)


def project_kernel(slots, chunks, first, last, *refs):
    parts = refs[: len(slots) * chunks]
    order, gain, weight_hbm = refs[len(slots) * chunks : len(slots) * chunks + 3]
    rest = list(refs[len(slots) * chunks + 3 : -2])
    weight, sems = refs[-2:]
    width = weight.shape[1]
    piece = width // chunks
    copies = []
    for i, m in enumerate(slots):
        rows = pl.ds(pl.multiple_of(order[m] * width, width), width)
        copies.append(
            pltpu.make_async_copy(weight_hbm.at[rows, :], weight.at[i], sems.at[i])
        )
        copies[-1].start()
    if first:
        total = squares = None
    else:
        total, squares = rest[0][...], rest[1][...]
        rest = rest[2:]
    for i, m in enumerate(slots):
        scale = gain[pl.ds(order[m], 1), :]
        copies[i].wait()
        for c in range(chunks):
            wide = parts[i * chunks + c][...].astype(jnp.float32)
            for lane in range(0, piece, HD):
                tile = wide[:, lane : lane + HD]
                squares = tile * tile if squares is None else squares + tile * tile
            scaled = (wide * scale[:, c * piece : (c + 1) * piece]).astype(jnp.bfloat16)
            term = jnp.dot(
                scaled,
                weight[i, c * piece : (c + 1) * piece, :],
                preferred_element_type=jnp.float32,
            )
            total = term if total is None else total + term
    if not last:
        rest[0][...] = total
        rest[1][...] = squares
        return
    select, out = rest
    inverse = lax.rsqrt(jnp.sum(squares, axis=1, keepdims=True) / D + 1e-05)
    projected = (total * inverse).astype(jnp.bfloat16)
    out[...] = jnp.dot(select[...], projected, preferred_element_type=jnp.float32).astype(
        jnp.bfloat16
    )


def project(slots, parts, order, gain, weight, before, select):
    chunks = len(parts) // len(slots)
    live = parts[0].shape[0]
    width = gain.shape[1]
    columns = weight.shape[1]
    first = before is None
    last = select is not None
    operands = list(parts) + [order, gain, weight]
    specs = [VMEM] * len(parts) + [SMEM, VMEM, ANY]
    if not first:
        operands += list(before)
        specs += [VMEM, VMEM]
    if last:
        operands.append(select)
        specs.append(VMEM)
        out_shape = jax.ShapeDtypeStruct((select.shape[0], columns), jnp.bfloat16)
        out_specs = VMEM
    else:
        out_shape = [
            jax.ShapeDtypeStruct((live, columns), jnp.float32),
            jax.ShapeDtypeStruct((live, HD), jnp.float32),
        ]
        out_specs = [VMEM, VMEM]
    return pl.pallas_call(
        functools.partial(project_kernel, tuple(slots), chunks, first, last),
        out_shape=out_shape,
        in_specs=specs,
        out_specs=out_specs,
        scratch_shapes=[
            pltpu.VMEM((len(slots), width, columns), jnp.bfloat16),
            pltpu.SemaphoreType.DMA((len(slots),)),
        ],
        cost_estimate=pl.CostEstimate(
            flops=2 * live * len(slots) * width * columns,
            bytes_accessed=2 * len(slots) * width * (columns + live),
            transcendentals=0,
        ),
        name="project_last" if last else "project",
    )(*operands)


def regroup_table(counts, owners, my_index, devices, live):
    slot_rows = jnp.arange(CAP, dtype=jnp.int32)
    starts = jnp.cumsum(counts) - counts
    kv_group = my_index // (devices // KVH)
    column_owner = lax.dynamic_index_in_dim(owners, kv_group, 1, keepdims=False)
    device_ids = jnp.arange(devices, dtype=jnp.int32)
    member = column_owner[None, :] == device_ids[:, None]
    ranking = jnp.cumsum(member.astype(jnp.int32), axis=1) - 1
    slot_ids = jnp.arange(OWN_G, dtype=jnp.int32)
    chosen = member[None, :, :] & (ranking[None, :, :] == slot_ids[:, None, None])
    chosen = chosen.astype(jnp.int32)
    begin = jnp.sum(chosen * starts[None, None, :], axis=2)
    size = jnp.sum(chosen * counts[None, None, :], axis=2)
    source = jnp.where(
        slot_rows[None, :, None] < size[:, None, :],
        begin[:, None, :] + slot_rows[None, :, None],
        -1,
    ).reshape(OWN_G * CAP * devices)
    live_ids = jnp.arange(live, dtype=jnp.int32)
    return (source[:, None] == live_ids[None, :]).astype(jnp.bfloat16)


def body(
    queries, prefix_kv, suffix_kv, counts, residual, out_weight, norm_gain, qkv_weight, owners
):
    devices = lax.axis_size("wide")
    my_index = lax.axis_index("wide")
    n, step, order_table = ring_plan(devices)
    order = lax.dynamic_index_in_dim(jnp.asarray(order_table), my_index, 0, keepdims=False)
    live = devices * MEAN_LIVE
    width = residual.shape[1]
    columns = qkv_weight.shape[1]
    chunks = 2 if width % (2 * HD) == 0 else 1

    gathered = []
    for half in range(HALVES):
        block = attend(half, queries, prefix_kv, suffix_kv)
        gathered.append(ring_gather(block, n, step, half % 2 == 0)[0])
    before = mix(0, gathered[0], out_weight, (), chunks)
    packed = mix(1, gathered[1], out_weight, (before, order, counts, residual), chunks)

    select = regroup_table(counts, owners, my_index, devices, live)
    rings = [ring_gather(part, n, step, i % 2 == 0) for i, part in enumerate(packed)]
    gain = norm_gain.reshape(devices, width)
    distances = [[0]]
    for s in range(1, n // 2 + 1):
        distances.append(sorted({s, n - s}))
    carried = None
    for i, ks in enumerate(distances):
        slots = [2 * k + t for k in ks for t in range(2)]
        parts = [ring[0][m] for m in slots for ring in rings]
        last = i == len(distances) - 1
        carried = project(slots, parts, order, gain, qkv_weight, carried, select if last else None)
    outgoing = carried.reshape(OWN_G, CAP, devices, columns)
    incoming = lax.all_to_all(outgoing, "wide", split_axis=2, concat_axis=2, tiled=True)
    return incoming.reshape(1, OWN_G, CAP, KVH, GCOLS)


def solution(mesh):
    placed = (
        P(("groups", "wide"), None, None),
        P(("groups", "wide"), None, None, None),
        P(("groups", "wide"), None, None, None, None),
        P("groups"),
        P("groups", "wide"),
        P(None, "wide"),
        P(),
        P(None, "wide"),
        P(),
    )
    return jax.shard_map(
        body,
        mesh=mesh,
        in_specs=placed,
        out_specs=P(("groups", "wide"), None, None, None, None),
        check_vma=False,
    )
```

```python
import functools

import jax
import jax.numpy as jnp
from jax import lax
from jax.experimental import pallas as pl
from jax.experimental.pallas import tpu as pltpu
from jax.sharding import PartitionSpec as P

KVH = 8
HD = 128
D = 8192
GQ = 8
GCOLS = 1280
CTX = 1024
SUF = 64
CAP = 12
OWN_G = 2
MEAN_LIVE = 8

HALVES = 2
HALF_G = KVH // HALVES
PAD = 16
LOG2E = 1.4426950408889634


ANY = pl.BlockSpec(memory_space=pl.ANY)
SMEM = pl.BlockSpec(memory_space=pltpu.SMEM)
VMEM = pl.BlockSpec(memory_space=pltpu.VMEM)
MIB = 1 << 20


def near(x):
    return pltpu.with_memory_space_constraint(x, pltpu.VMEM)


def far(x):
    return pltpu.with_memory_space_constraint(x, pltpu.HBM)


def room(mib):
    return pltpu.CompilerParams(vmem_limit_bytes=mib * MIB)


def snake(chips):
    return chips <= 8 and chips % 2 == 0


def chip_ring(devices):
    chips = devices // 2
    if snake(chips):
        return list(range(0, chips, 2)) + list(range(chips - 1, 0, -2))
    return list(range(chips))


def ring_plan(devices):
    ring = chip_ring(devices)
    n = len(ring)
    step = {}
    for name, d in (("up", 1), ("down", -1)):
        step[name] = [
            (ring[k] * 2 + c, ring[(k + d) % n] * 2 + c) for k in range(n) for c in range(2)
        ]
    step["swap"] = [(i, i ^ 1) for i in range(devices)]
    return n, step


def slot_owner(devices, m):
    chips = devices // 2
    me = lax.axis_index("wide")
    chip, core = me // 2, me % 2
    if snake(chips):
        at = jnp.where(chip % 2 == 0, chip // 2, chips - 1 - chip // 2)
    else:
        at = chip
    there = (at + m // 2) % chips
    if snake(chips):
        there = jnp.where(there < chips // 2, 2 * there, 2 * (chips - 1 - there) + 1)
    return 2 * there + (core + m) % 2


def ring_gather(block, n, step, long_up):
    pieces = [None] * n
    pieces[0] = block
    up = down = block
    up_steps = n // 2 if long_up else (n - 1) // 2
    down_steps = n - 1 - up_steps
    for s in range(1, max(up_steps, down_steps) + 1):
        if s <= up_steps:
            up = pieces[n - s] = lax.ppermute(up, "wide", step["up"])
        if s <= down_steps:
            down = pieces[s] = lax.ppermute(down, "wide", step["down"])
    both = []
    for piece in pieces:
        both += [piece, lax.ppermute(piece, "wide", step["swap"])]
    return both


def plan_kernel(
    devices, counts, owners, gain, select, pack, spread, scale, starts, begin, size, seen, table
):
    live = devices * MEAN_LIVE
    rows = devices * PAD
    blocks = devices * OWN_G

    def clear(i, carry):
        size[i] = 0
        begin[i] = 0
        seen[i // OWN_G] = 0
        return carry

    lax.fori_loop(0, blocks, clear, 0)
    kv_group = lax.axis_index("wide") // (devices // KVH)

    def visit(p, running):
        starts[p] = running
        owner = owners[kv_group, p]
        nth = seen[owner]
        seen[owner] = nth + 1

        @pl.when(nth < OWN_G)
        def _():
            begin[owner * OWN_G + nth] = running
            size[owner * OWN_G + nth] = counts[p]

        return running + counts[p]

    lax.fori_loop(0, devices, visit, jnp.int32(0))
    lane = lax.broadcasted_iota(jnp.int32, (CAP, live), 1)
    row = lax.broadcasted_iota(jnp.int32, (CAP, live), 0)
    for i in range(blocks):
        hit = (lane == begin[i] + row) & (row < size[i])
        table[i * CAP : (i + 1) * CAP, :] = hit.astype(jnp.float32)
    select[...] = table[...].astype(jnp.bfloat16)
    lane_slot = lax.broadcasted_iota(jnp.int32, (1, rows), 1) // PAD
    lane_row = lax.broadcasted_iota(jnp.int32, (1, rows), 1) % PAD
    place = jnp.full((1, rows), -1, jnp.int32)
    width = scale.shape[1]
    source = lax.broadcasted_iota(jnp.int32, (PAD, devices * CAP), 1)
    slot_row = lax.broadcasted_iota(jnp.int32, (PAD, devices * CAP), 0)
    for m in range(devices):
        parent = slot_owner(devices, m)
        place = jnp.where(
            (lane_slot == m) & (lane_row < counts[parent]), starts[parent] + lane_row, place
        )
        hit = (source == parent * CAP + slot_row) & (slot_row < CAP)
        spread[m * PAD : (m + 1) * PAD, :] = hit.astype(jnp.float32).astype(jnp.bfloat16)
        scale[m : m + 1, :] = gain[pl.ds(pl.multiple_of(parent * width, width), width)].reshape(
            1, width
        )
    hit = place == lax.broadcasted_iota(jnp.int32, (live, rows), 0)
    pack[...] = hit.astype(jnp.float32).astype(jnp.bfloat16)


def plan(counts, owners, norm_gain, devices, width):
    live = devices * MEAN_LIVE
    rows = devices * PAD
    blocks = devices * OWN_G
    return pl.pallas_call(
        functools.partial(plan_kernel, devices),
        out_shape=[
            pltpu.VMEM((blocks * CAP, live), jnp.bfloat16),
            pltpu.VMEM((live, rows), jnp.bfloat16),
            pltpu.VMEM((rows, devices * CAP), jnp.bfloat16),
            pltpu.VMEM((devices, width), jnp.float32),
        ],
        in_specs=[SMEM, SMEM, VMEM],
        out_specs=[VMEM] * 4,
        scratch_shapes=[
            pltpu.SMEM((devices,), jnp.int32),
            pltpu.SMEM((blocks,), jnp.int32),
            pltpu.SMEM((blocks,), jnp.int32),
            pltpu.SMEM((devices,), jnp.int32),
            pltpu.VMEM((blocks * CAP, live), jnp.float32),
        ],
        compiler_params=room(2 if devices <= 16 else 16),
        cost_estimate=pl.CostEstimate(flops=1000000, bytes_accessed=1000000, transcendentals=0),
        name="plan",
    )(counts, owners.T, norm_gain)


def attend_kernel(
    half, q_ref, kv_hbm, suffix_hbm, weight_hbm, out_ref, held, kv, suffix, heads, sems, held_sem
):
    copies = []
    for g in range(HALF_G):
        columns = pl.ds((half * HALF_G + g) * HD, HD)
        copies.append(
            (
                pltpu.make_async_copy(kv_hbm.at[0, :, :, columns], kv.at[g], sems.at[g, 0]),
                pltpu.make_async_copy(
                    suffix_hbm.at[0, :, :, :, columns], suffix.at[g], sems.at[g, 1]
                ),
            )
        )
        for copy in copies[-1]:
            copy.start()
    hold = pltpu.make_async_copy(weight_hbm, held, held_sem)
    hold.start()
    heads[...] = jnp.zeros_like(heads)
    rows = GQ * PAD
    own_row = lax.broadcasted_iota(jnp.int32, (rows, CAP * SUF), 0) % PAD
    own_key = lax.broadcasted_iota(jnp.int32, (rows, CAP * SUF), 1) // SUF
    mine = own_row == own_key
    scale = HD ** (-0.5) * LOG2E
    contract = (((1,), (1,)), ((), ()))
    for g in range(HALF_G):
        for q in range(GQ):
            col = (g * GQ + q) * HD
            heads[q * PAD : q * PAD + CAP, :] = q_ref[0, :, col : col + HD]
        for copy in copies[g]:
            copy.wait()
        query = heads[...]
        distant = lax.dot_general(query, kv[g, 0], contract, preferred_element_type=jnp.float32)
        nearby = lax.dot_general(
            query,
            suffix[g, :, 0].reshape(CAP * SUF, HD),
            contract,
            preferred_element_type=jnp.float32,
        )
        nearby = jnp.where(mine, nearby, -1e30)
        top = jnp.maximum(
            jnp.max(distant, axis=1, keepdims=True), jnp.max(nearby, axis=1, keepdims=True)
        )
        distant = jnp.exp2((distant - top) * scale)
        nearby = jnp.exp2((nearby - top) * scale)
        total = jnp.sum(distant, axis=1, keepdims=True) + jnp.sum(nearby, axis=1, keepdims=True)
        mixed = jnp.dot(distant.astype(jnp.bfloat16), kv[g, 1], preferred_element_type=jnp.float32)
        mixed = mixed + jnp.dot(
            nearby.astype(jnp.bfloat16),
            suffix[g, :, 1].reshape(CAP * SUF, HD),
            preferred_element_type=jnp.float32,
        )
        mixed = (mixed / total).astype(jnp.bfloat16)
        for q in range(GQ):
            out_ref[g * CAP : (g + 1) * CAP, q * HD : (q + 1) * HD] = mixed[
                q * PAD : q * PAD + CAP, :
            ]
    hold.wait()


def attend(half, queries, prefix_kv, suffix_kv, weight):
    columns = HALF_G * GQ * HD
    keys = CTX + CAP * SUF
    return pl.pallas_call(
        functools.partial(attend_kernel, half),
        out_shape=[
            pltpu.VMEM((HALF_G * CAP, GQ * HD), jnp.bfloat16),
            pltpu.VMEM(weight.shape, weight.dtype),
        ],
        grid=(1,),
        in_specs=[pl.BlockSpec((1, CAP, columns), lambda i: (0, 0, half)), ANY, ANY, ANY],
        out_specs=[VMEM, ANY],
        scratch_shapes=[
            pltpu.VMEM((HALF_G, 2, CTX, HD), jnp.bfloat16),
            pltpu.VMEM((HALF_G, CAP, 2, SUF, HD), jnp.bfloat16),
            pltpu.VMEM((GQ * PAD, HD), jnp.bfloat16),
            pltpu.SemaphoreType.DMA((HALF_G, 2)),
            pltpu.SemaphoreType.DMA,
        ],
        cost_estimate=pl.CostEstimate(
            flops=4 * HALF_G * GQ * PAD * keys * HD,
            bytes_accessed=4 * HALF_G * keys * HD,
            transcendentals=HALF_G * GQ * PAD * keys,
        ),
        compiler_params=room(8),
        name=f"attend_{half}",
    )(queries, far(prefix_kv), far(suffix_kv), far(weight))


def mix_kernel(half, slots, *refs):
    pieces = refs[:slots]
    weight = refs[slots]
    lhs = refs[-1]
    depth = GQ * HD
    total = None
    lhs[...] = jnp.zeros_like(lhs)
    for g in range(HALF_G):
        for m in range(slots):
            lhs[m * PAD : m * PAD + CAP, :] = pieces[m][g * CAP : (g + 1) * CAP, :]
        first = (half * HALF_G + g) * depth
        term = jnp.dot(
            lhs[...], weight[first : first + depth, :], preferred_element_type=jnp.float32
        )
        total = term if total is None else total + term
    if half < HALVES - 1:
        refs[slots + 1][...] = total
        return
    before, pack, spread, residual = refs[slots + 1 : slots + 5]
    outs = refs[slots + 5 : -1]
    ordered = jnp.dot(spread[...], residual[...], preferred_element_type=jnp.float32)
    stream = (ordered + (before[...] + total)).astype(jnp.bfloat16)
    packed = jnp.dot(
        pack[...], stream, preferred_element_type=jnp.float32
    ).astype(jnp.bfloat16)
    width = packed.shape[1] // len(outs)
    for i, out in enumerate(outs):
        out[...] = packed[:, i * width : (i + 1) * width]


def mix(half, pieces, out_weight, extra, chunks):
    slots = len(pieces)
    width = out_weight.shape[1]
    rows = slots * PAD
    last = half == HALVES - 1
    depth = GQ * HD
    if last:
        live = slots * MEAN_LIVE
        out_shape = [pltpu.VMEM((live, width // chunks), jnp.bfloat16)] * chunks
        extra_specs = [VMEM] * 4
    else:
        out_shape = pltpu.VMEM((rows, width), jnp.float32)
        extra_specs = []
    return pl.pallas_call(
        functools.partial(mix_kernel, half, slots),
        out_shape=out_shape,
        in_specs=[VMEM] * slots + [VMEM] + extra_specs,
        out_specs=[VMEM] * chunks if last else VMEM,
        scratch_shapes=[pltpu.VMEM((rows, depth), jnp.bfloat16)],
        cost_estimate=pl.CostEstimate(
            flops=2 * rows * HALF_G * depth * width,
            bytes_accessed=2 * HALF_G * depth * (width + slots * CAP),
            transcendentals=0,
        ),
        compiler_params=room(8 if slots <= 16 else 32),
        name=f"mix_{half}",
    )(*[near(piece) for piece in pieces], near(out_weight), *extra)


def project_kernel(devices, slots, chunks, first, last, *refs):
    parts = refs[: len(slots) * chunks]
    gain, weight = refs[len(slots) * chunks : len(slots) * chunks + 2]
    rest = list(refs[len(slots) * chunks + 2 :])
    width = gain.shape[1]
    piece = width // chunks
    if first:
        total = squares = None
    else:
        total, squares = rest[0][...], rest[1][...]
        rest = rest[2:]
    for i, m in enumerate(slots):
        scale = gain[m : m + 1, :]
        owner = slot_owner(devices, m)
        for c in range(chunks):
            rows = pl.ds(pl.multiple_of(owner * width + c * piece, piece), piece)
            wide = parts[i * chunks + c][...].astype(jnp.float32)
            for lane in range(0, piece, HD):
                tile = wide[:, lane : lane + HD]
                squares = tile * tile if squares is None else squares + tile * tile
            scaled = (wide * scale[:, c * piece : (c + 1) * piece]).astype(jnp.bfloat16)
            term = jnp.dot(
                scaled,
                weight[rows, :],
                preferred_element_type=jnp.float32,
            )
            total = term if total is None else total + term
    if not last:
        rest[0][...] = total
        rest[1][...] = squares
        return
    select, out = rest
    inverse = lax.rsqrt(jnp.sum(squares, axis=1, keepdims=True) / D + 1e-05)
    projected = (total * inverse).astype(jnp.bfloat16)
    out[...] = jnp.dot(select[...], projected, preferred_element_type=jnp.float32).astype(
        jnp.bfloat16
    )


def project(slots, parts, gain, weight, before, select):
    chunks = len(parts) // len(slots)
    live = parts[0].shape[0]
    width = gain.shape[1]
    columns = weight.shape[1]
    first = before is None
    last = select is not None
    operands = [near(part) for part in parts] + [near(gain), near(weight)]
    specs = [VMEM] * len(parts) + [VMEM, VMEM]
    if not first:
        operands += [near(x) for x in before]
        specs += [VMEM, VMEM]
    if last:
        operands.append(near(select))
        specs.append(VMEM)
        out_shape = jax.ShapeDtypeStruct((select.shape[0], columns), jnp.bfloat16)
        out_specs = VMEM
    else:
        out_shape = [
            pltpu.VMEM((live, columns), jnp.float32),
            pltpu.VMEM((live, HD), jnp.float32),
        ]
        out_specs = [VMEM, VMEM]
    return pl.pallas_call(
        functools.partial(project_kernel, gain.shape[0], tuple(slots), chunks, first, last),
        out_shape=out_shape,
        in_specs=specs,
        out_specs=out_specs,
        cost_estimate=pl.CostEstimate(
            flops=2 * live * len(slots) * width * columns,
            bytes_accessed=2 * len(slots) * width * (columns + live),
            transcendentals=0,
        ),
        compiler_params=room(4 if live <= 128 else 12),
        name="project_last" if last else "project",
    )(*operands)


def body(
    queries, prefix_kv, suffix_kv, counts, residual, out_weight, norm_gain, qkv_weight, owners
):
    devices = lax.axis_size("wide")
    n, step = ring_plan(devices)
    width = residual.shape[1]
    columns = qkv_weight.shape[1]
    chunks = 2 if width % (2 * HD) == 0 else 1

    gathered = []
    held = []
    for half, weight in enumerate((out_weight, qkv_weight)):
        block, on_chip = attend(half, queries, prefix_kv, suffix_kv, weight)
        held.append(on_chip)
        gathered.append(ring_gather(block, n, step, half % 2 == 0))
    out_weight, qkv_weight = held
    select, pack, spread, gain = plan(counts, owners, norm_gain, devices, width)
    before = mix(0, gathered[0], out_weight, (), chunks)
    packed = mix(1, gathered[1], out_weight, (near(before), near(pack), near(spread), residual), chunks)

    ups, downs = list(packed), list(packed)
    arrived = [{0: part} for part in packed]
    swapped = [{0: lax.ppermute(part, "wide", step["swap"])} for part in packed]
    carried = None
    done = []
    for s in range(n // 2 + 1):
        if s > 0:
            for i in range(chunks):
                if s >= 2:
                    ups[i], downs[i], _ = lax.optimization_barrier((ups[i], downs[i], done[s - 2]))
                if s < n - s or i % 2 == 0 or chunks == 1:
                    ups[i] = arrived[i][n - s] = lax.ppermute(ups[i], "wide", step["up"])
                if s < n - s or (i % 2 == 1 and chunks > 1):
                    downs[i] = arrived[i][s] = lax.ppermute(downs[i], "wide", step["down"])
            for i in range(chunks):
                for k in sorted({s, n - s}):
                    swapped[i][k] = lax.ppermute(arrived[i][k], "wide", step["swap"])
        ks = sorted({s, n - s} - {n})
        slots = [2 * k + t for k in ks for t in range(2)]
        parts = [(swapped if m % 2 else arrived)[i][m // 2] for m in slots for i in range(chunks)]
        last = s == n // 2
        carried = project(slots, parts, gain, qkv_weight, carried, select if last else None)
        if not last:
            done.append(carried[1])
    outgoing = carried.reshape(devices, OWN_G * CAP, columns)
    incoming = lax.all_to_all(outgoing, "wide", split_axis=0, concat_axis=0, tiled=True)
    return incoming.transpose(1, 0, 2).reshape(1, OWN_G, CAP, KVH, GCOLS)


def solution(mesh):
    placed = (
        P(("groups", "wide"), None, None),
        P(("groups", "wide"), None, None, None),
        P(("groups", "wide"), None, None, None, None),
        P("groups"),
        P("groups", "wide"),
        P(None, "wide"),
        P(),
        P(None, "wide"),
        P(),
    )
    return jax.shard_map(
        body,
        mesh=mesh,
        in_specs=placed,
        out_specs=P(("groups", "wide"), None, None, None, None),
        check_vma=False,
    )
```

```python
import functools

import jax
import jax.numpy as jnp
from jax import lax
from jax.experimental import pallas as pl
from jax.experimental.pallas import tpu as pltpu
from jax.sharding import PartitionSpec as P

KVH = 8
HD = 128
D = 8192
GQ = 8
GCOLS = 1280
CTX = 1024
SUF = 64
CAP = 12
OWN_G = 2
MEAN_LIVE = 8

HALVES = 2
HALF_G = KVH // HALVES
PAD = 16
LOG2E = 1.4426950408889634


ANY = pl.BlockSpec(memory_space=pl.ANY)
SMEM = pl.BlockSpec(memory_space=pltpu.SMEM)
VMEM = pl.BlockSpec(memory_space=pltpu.VMEM)
MIB = 1 << 20


def near(x):
    return pltpu.with_memory_space_constraint(x, pltpu.VMEM)


def far(x):
    return pltpu.with_memory_space_constraint(x, pltpu.HBM)


def room(mib):
    return pltpu.CompilerParams(vmem_limit_bytes=mib * MIB)


def snake(chips):
    return chips <= 8 and chips % 2 == 0


def ring_moves(devices):
    chips = devices // 2
    ring = list(range(chips))
    if snake(chips):
        ring = list(range(0, chips, 2)) + list(range(chips - 1, 0, -2))
    forward = [(2 * ring[k], 2 * ring[(k + 1) % chips]) for k in range(chips)]
    backward = [(2 * ring[k] + 1, 2 * ring[k - 1] + 1) for k in range(chips)]
    return forward + backward, [(i, i ^ 1) for i in range(devices)]


def slot_owner(devices, m):
    chips = devices // 2
    bundle, second = m // 2, m % 2
    distance, swapped = (bundle + 1) // 2, bundle > 0 and bundle % 2 == 0
    me = lax.axis_index("wide")
    chip, core = me // 2, me % 2
    at = chip
    if snake(chips):
        at = jnp.where(chip % 2 == 0, chip // 2, chips - 1 - chip // 2)
    sign = (2 * core - 1) * (-1 if swapped else 1)
    there = (at + sign * distance + chips) % chips
    if snake(chips):
        there = jnp.where(there < chips // 2, 2 * there, 2 * (chips - 1 - there) + 1)
    return 2 * there + (core + second + (1 if swapped else 0)) % 2


def join_kernel(first, second, out):
    rows = first.shape[0]
    out[:rows, :] = first[...]
    out[rows:, :] = second[...]


def ring_gather(block, devices):
    chips = devices // 2
    step, swap = ring_moves(devices)
    other = lax.ppermute(block, "wide", swap)
    rows, columns = block.shape
    bundle = pl.pallas_call(
        join_kernel,
        out_shape=pltpu.VMEM((2 * rows, columns), block.dtype),
        in_specs=[VMEM, VMEM],
        out_specs=VMEM,
        compiler_params=room(1),
        name="join",
    )(near(block), near(other))
    bundles = [bundle]
    for distance in range(1, chips // 2 + 1):
        bundle = lax.ppermute(bundle, "wide", step)
        bundles.append(bundle)
        if distance < chips // 2:
            bundles.append(lax.ppermute(bundle, "wide", swap))
    return bundles


def plan_kernel(
    devices,
    counts,
    owners,
    gain,
    select,
    pack,
    spread,
    scale,
    starts,
    begin,
    size,
    seen,
    table,
):
    live = devices * MEAN_LIVE
    rows = devices * PAD
    blocks = devices * OWN_G

    def clear(i, carry):
        size[i] = 0
        begin[i] = 0
        seen[i // OWN_G] = 0
        return carry

    lax.fori_loop(0, blocks, clear, 0)
    kv_group = lax.axis_index("wide") // (devices // KVH)

    def visit(p, running):
        starts[p] = running
        owner = owners[kv_group, p]
        nth = seen[owner]
        seen[owner] = nth + 1

        @pl.when(nth < OWN_G)
        def _():
            begin[owner * OWN_G + nth] = running
            size[owner * OWN_G + nth] = counts[p]

        return running + counts[p]

    lax.fori_loop(0, devices, visit, jnp.int32(0))
    lane = lax.broadcasted_iota(jnp.int32, (CAP, live), 1)
    row = lax.broadcasted_iota(jnp.int32, (CAP, live), 0)
    for i in range(blocks):
        hit = (lane == begin[i] + row) & (row < size[i])
        table[i * CAP : (i + 1) * CAP, :] = hit.astype(jnp.float32)
    select[...] = table[...].astype(jnp.bfloat16)
    lane_slot = lax.broadcasted_iota(jnp.int32, (1, rows), 1) // PAD
    lane_row = lax.broadcasted_iota(jnp.int32, (1, rows), 1) % PAD
    place = jnp.full((1, rows), -1, jnp.int32)
    width = scale.shape[1]
    source = lax.broadcasted_iota(jnp.int32, (PAD, devices * CAP), 1)
    slot_row = lax.broadcasted_iota(jnp.int32, (PAD, devices * CAP), 0)
    for m in range(devices):
        parent = slot_owner(devices, m)
        place = jnp.where(
            (lane_slot == m) & (lane_row < counts[parent]), starts[parent] + lane_row, place
        )
        hit = (source == parent * CAP + slot_row) & (slot_row < CAP)
        spread[m * PAD : (m + 1) * PAD, :] = hit.astype(jnp.float32).astype(jnp.bfloat16)
        scale[m : m + 1, :] = gain[pl.ds(pl.multiple_of(parent * width, width), width)].reshape(
            1, width
        )
    hit = place == lax.broadcasted_iota(jnp.int32, (live, rows), 0)
    pack[...] = hit.astype(jnp.float32).astype(jnp.bfloat16)


def plan(counts, owners, norm_gain, devices, width):
    live = devices * MEAN_LIVE
    rows = devices * PAD
    blocks = devices * OWN_G
    return pl.pallas_call(
        functools.partial(plan_kernel, devices),
        out_shape=[
            pltpu.VMEM((blocks * CAP, live), jnp.bfloat16),
            pltpu.VMEM((live, rows), jnp.bfloat16),
            pltpu.VMEM((rows, devices * CAP), jnp.bfloat16),
            pltpu.VMEM((devices, width), jnp.float32),
        ],
        in_specs=[SMEM, SMEM, VMEM],
        out_specs=[VMEM] * 4,
        scratch_shapes=[
            pltpu.SMEM((devices,), jnp.int32),
            pltpu.SMEM((blocks,), jnp.int32),
            pltpu.SMEM((blocks,), jnp.int32),
            pltpu.SMEM((devices,), jnp.int32),
            pltpu.VMEM((blocks * CAP, live), jnp.float32),
        ],
        compiler_params=room(2 if devices <= 16 else 16),
        cost_estimate=pl.CostEstimate(flops=1000000, bytes_accessed=1000000, transcendentals=0),
        name="plan",
    )(counts, owners.T, norm_gain)


def attend_rows(query_rows, keys, values, suffix, tall, out_ref, ready):
    rows = CAP * GQ
    pair = 2 * SUF
    own_row = lax.broadcasted_iota(jnp.int32, (rows, pair), 0) // GQ
    own_key = lax.broadcasted_iota(jnp.int32, (rows, pair), 1) // SUF
    mine = [own_row == own_key + 2 * j for j in range(CAP // 2)]
    scale = HD ** (-0.5) * LOG2E
    contract = (((1,), (1,)), ((), ()))
    ready(0)
    for g in range(HALF_G):
        lanes = slice(g * HD, (g + 1) * HD)
        for q in range(GQ):
            col = (g * GQ + q) * HD
            tall[pl.ds(q, CAP, stride=GQ), :] = query_rows[:, col : col + HD].astype(jnp.float32)
        query = tall[...].astype(jnp.bfloat16)
        distant = lax.dot_general(query, keys[:, lanes], contract, preferred_element_type=jnp.float32)
        every = lax.dot_general(
            query,
            suffix[:, 0, :, lanes].reshape(CAP * SUF, HD),
            contract,
            preferred_element_type=jnp.float32,
        )
        nearby = jnp.full((rows, pair), -1e30, jnp.float32)
        for j in range(CAP // 2):
            nearby = jnp.where(mine[j], every[:, j * pair : (j + 1) * pair], nearby)
        top = jnp.maximum(
            jnp.max(distant, axis=1, keepdims=True), jnp.max(nearby, axis=1, keepdims=True)
        )
        distant = jnp.exp2((distant - top) * scale)
        nearby = jnp.exp2((nearby - top) * scale)
        total = jnp.sum(distant, axis=1, keepdims=True) + jnp.sum(nearby, axis=1, keepdims=True)
        if g == 0:
            ready(1)
        mixed = jnp.dot(distant.astype(jnp.bfloat16), values[:, lanes], preferred_element_type=jnp.float32)
        wide = jnp.concatenate(
            [jnp.where(mine[j], nearby, 0.0).astype(jnp.bfloat16) for j in range(CAP // 2)], axis=1
        )
        mixed = mixed + jnp.dot(
            wide,
            suffix[:, 1, :, lanes].reshape(CAP * SUF, HD),
            preferred_element_type=jnp.float32,
        )
        tall[...] = mixed / total
        for q in range(GQ):
            out_ref[g * CAP : (g + 1) * CAP, q * HD : (q + 1) * HD] = tall[
                pl.ds(q, CAP, stride=GQ), :
            ].astype(jnp.bfloat16)


def attend_first_kernel(
    q_hbm, kv_hbm, suffix_hbm, out_ref, q_next, kv_next, suffix_next, q, kv, suffix, tall, sems
):
    columns = HALF_G * GQ * HD
    lanes = HALF_G * HD

    def part(half, q_to, kv_to, suffix_to, base):
        heads, spots = pl.ds(half * columns, columns), pl.ds(half * lanes, lanes)
        moves = [
            (q_hbm.at[0, :, heads], q_to),
            (kv_hbm.at[0, 0, :, spots], kv_to.at[0]),
            (suffix_hbm.at[0, :, :, :, spots], suffix_to),
            (kv_hbm.at[0, 1, :, spots], kv_to.at[1]),
        ]
        copies = [
            pltpu.make_async_copy(source, target, sems.at[base + i])
            for i, (source, target) in enumerate(moves)
        ]
        for copy in copies:
            copy.start()
        return copies

    now = part(0, q, kv, suffix, 0)
    later = part(1, q_next, kv_next, suffix_next, 4)

    def ready(stage):
        for copy in now[3:] if stage else now[:3]:
            copy.wait()

    attend_rows(q, kv.at[0], kv.at[1], suffix, tall, out_ref, ready)
    for copy in later:
        copy.wait()


def attend_second_kernel(q, kv, suffix, out_ref, tall):
    attend_rows(q, kv.at[0], kv.at[1], suffix, tall, out_ref, lambda stage: None)


def attend_cost():
    keys = CTX + CAP * SUF
    return pl.CostEstimate(
        flops=4 * HALF_G * GQ * CAP * keys * HD,
        bytes_accessed=4 * HALF_G * keys * HD,
        transcendentals=HALF_G * GQ * CAP * (CTX + SUF),
    )


def attend_first(queries, prefix_kv, suffix_kv):
    block = pltpu.VMEM((HALF_G * CAP, GQ * HD), jnp.bfloat16)
    q = pltpu.VMEM((CAP, HALF_G * GQ * HD), jnp.bfloat16)
    kv = pltpu.VMEM((2, CTX, HALF_G * HD), jnp.bfloat16)
    suffix = pltpu.VMEM((CAP, 2, SUF, HALF_G * HD), jnp.bfloat16)
    return pl.pallas_call(
        attend_first_kernel,
        out_shape=[block, q, kv, suffix],
        in_specs=[ANY] * 3,
        out_specs=[VMEM] + [ANY] * 3,
        scratch_shapes=[
            q,
            kv,
            suffix,
            pltpu.VMEM((GQ * CAP, HD), jnp.float32),
            pltpu.SemaphoreType.DMA((8,)),
        ],
        cost_estimate=attend_cost(),
        compiler_params=room(8),
        name="attend_first",
    )(far(queries), far(prefix_kv), far(suffix_kv))


def attend_second(q, kv, suffix):
    return pl.pallas_call(
        attend_second_kernel,
        out_shape=pltpu.VMEM((HALF_G * CAP, GQ * HD), jnp.bfloat16),
        in_specs=[VMEM] * 3,
        out_specs=VMEM,
        scratch_shapes=[pltpu.VMEM((GQ * CAP, HD), jnp.float32)],
        cost_estimate=attend_cost(),
        compiler_params=room(6),
        name="attend_second",
    )(near(q), near(kv), near(suffix))


def mix_kernel(half, slots, *refs):
    pieces = refs[: slots // 2]
    refs = refs[slots // 2 :]
    weight, lhs = refs[0], refs[-1]
    refs = refs[1:-1]
    depth = GQ * HD
    total = None
    lhs[...] = jnp.zeros_like(lhs)
    for g in range(HALF_G):
        for m in range(slots):
            row = (m % 2 * HALF_G + g) * CAP
            lhs[m * PAD : m * PAD + CAP, :] = pieces[m // 2][row : row + CAP, :]
        first = (half * HALF_G + g) * depth
        term = jnp.dot(
            lhs[...], weight[first : first + depth, :], preferred_element_type=jnp.float32
        )
        total = term if total is None else total + term
    if half < HALVES - 1:
        refs[0][...] = total
        return
    before, pack, spread, residual = refs[:4]
    outs = refs[4:]
    ordered = jnp.dot(spread[...], residual[...], preferred_element_type=jnp.float32)
    stream = (ordered + (before[...] + total)).astype(jnp.bfloat16)
    packed = jnp.dot(
        pack[...], stream, preferred_element_type=jnp.float32
    ).astype(jnp.bfloat16)
    width = packed.shape[1] // len(outs)
    for i, out in enumerate(outs):
        out[...] = packed[:, i * width : (i + 1) * width]


def mix(half, pieces, out_weight, extra, chunks):
    slots = 2 * len(pieces)
    width = out_weight.shape[1]
    rows = slots * PAD
    last = half == HALVES - 1
    depth = GQ * HD
    if last:
        live = slots * MEAN_LIVE
        out_shape = [pltpu.VMEM((live, width // chunks), jnp.bfloat16)] * chunks
    else:
        out_shape = [pltpu.VMEM((rows, width), jnp.float32)]
    operands = [near(piece) for piece in pieces] + [near(out_weight)]
    operands += list(extra)
    return pl.pallas_call(
        functools.partial(mix_kernel, half, slots),
        out_shape=out_shape,
        in_specs=[VMEM] * len(operands),
        out_specs=[VMEM] * len(out_shape),
        scratch_shapes=[pltpu.VMEM((rows, depth), jnp.bfloat16)],
        cost_estimate=pl.CostEstimate(
            flops=2 * rows * HALF_G * depth * width,
            bytes_accessed=2 * HALF_G * depth * (width + slots * CAP),
            transcendentals=0,
        ),
        compiler_params=room(8 if slots <= 16 else 32),
        name=f"mix_{half}",
    )(*operands)


def project_kernel(devices, spans, chunks, first, last, *refs):
    parts = refs[: len(spans) * chunks]
    gain, weight = refs[len(spans) * chunks : len(spans) * chunks + 2]
    rest = list(refs[len(spans) * chunks + 2 :])
    width = gain.shape[1]
    piece = width // chunks
    live = parts[0].shape[0] // 2
    if first:
        total = squares = None
    else:
        total, squares = rest[0][...], rest[1][...]
        rest = rest[2:]
    for i, q in enumerate(spans):
        for t in range(2):
            m = 2 * q + t
            scale = gain[m : m + 1, :]
            owner = slot_owner(devices, m)
            for c in range(chunks):
                rows = pl.ds(pl.multiple_of(owner * width + c * piece, piece), piece)
                wide = parts[i * chunks + c][t * live : (t + 1) * live, :].astype(jnp.float32)
                for lane in range(0, piece, HD):
                    tile = wide[:, lane : lane + HD]
                    squares = tile * tile if squares is None else squares + tile * tile
                scaled = (wide * scale[:, c * piece : (c + 1) * piece]).astype(jnp.bfloat16)
                term = jnp.dot(scaled, weight[rows, :], preferred_element_type=jnp.float32)
                total = term if total is None else total + term
    if not last:
        rest[0][...] = total
        rest[1][...] = squares
        return
    select, out = rest
    inverse = lax.rsqrt(jnp.sum(squares, axis=1, keepdims=True) / D + 1e-05)
    projected = (total * inverse).astype(jnp.bfloat16)
    out[...] = jnp.dot(select[...], projected, preferred_element_type=jnp.float32).astype(
        jnp.bfloat16
    )


def project(spans, parts, gain, weight, before, select):
    chunks = len(parts) // len(spans)
    live = parts[0].shape[0] // 2
    width = gain.shape[1]
    columns = weight.shape[1]
    first = before is None
    last = select is not None
    operands = [near(part) for part in parts] + [near(gain), near(weight)]
    specs = [VMEM] * len(parts) + [VMEM, VMEM]
    if not first:
        operands += [near(x) for x in before]
        specs += [VMEM, VMEM]
    if last:
        operands.append(near(select))
        specs.append(VMEM)
        out_shape = jax.ShapeDtypeStruct((select.shape[0], columns), jnp.bfloat16)
        out_specs = VMEM
    else:
        out_shape = [
            pltpu.VMEM((live, columns), jnp.float32),
            pltpu.VMEM((live, HD), jnp.float32),
        ]
        out_specs = [VMEM, VMEM]
    return pl.pallas_call(
        functools.partial(project_kernel, gain.shape[0], tuple(spans), chunks, first, last),
        out_shape=out_shape,
        in_specs=specs,
        out_specs=out_specs,
        cost_estimate=pl.CostEstimate(
            flops=4 * live * len(spans) * width * columns,
            bytes_accessed=4 * len(spans) * width * (columns + live),
            transcendentals=0,
        ),
        compiler_params=room(4 if live <= 128 else 12),
        name="project_last" if last else "project",
    )(*operands)


def body(
    queries, prefix_kv, suffix_kv, counts, residual, out_weight, norm_gain, qkv_weight, owners
):
    devices = lax.axis_size("wide")
    width = residual.shape[1]
    columns = qkv_weight.shape[1]
    chunks = 2 if width % (2 * HD) == 0 else 1

    out_weight, qkv_weight = near(out_weight), near(qkv_weight)
    first, *rest = attend_first(queries, prefix_kv, suffix_kv)
    first = ring_gather(first, devices)
    second = ring_gather(attend_second(*rest), devices)
    select, pack, spread, gain = plan(counts, owners, norm_gain, devices, width)
    (before,) = mix(0, first, out_weight, (), chunks)
    extra = (near(before), near(pack), near(spread), near(residual))
    packed = mix(1, second, out_weight, extra, chunks)

    parts = [ring_gather(part, devices) for part in packed]
    chips = devices // 2
    middle = (chips - 1) // 2
    carried = None
    for spans in (range(middle), range(middle, chips - 1), range(chips - 1, chips)):
        blocks = [chunk[q] for q in spans for chunk in parts]
        last = spans[-1] == chips - 1
        carried = project(
            spans, blocks, gain, qkv_weight, carried, select if last else None
        )
    outgoing = carried.reshape(devices, OWN_G * CAP, columns)
    incoming = lax.all_to_all(outgoing, "wide", split_axis=0, concat_axis=0, tiled=True)
    return incoming.transpose(1, 0, 2).reshape(1, OWN_G, CAP, KVH, GCOLS)


def solution(mesh):
    placed = (
        P(("groups", "wide"), None, None),
        P(("groups", "wide"), None, None, None),
        P(("groups", "wide"), None, None, None, None),
        P("groups"),
        P("groups", "wide"),
        P(None, "wide"),
        P(),
        P(None, "wide"),
        P(),
    )
    return jax.shard_map(
        body,
        mesh=mesh,
        in_specs=placed,
        out_specs=P(("groups", "wide"), None, None, None, None),
        check_vma=False,
    )
```

```python
import functools

import jax
import jax.numpy as jnp
from jax import lax
from jax.experimental import pallas as pl
from jax.experimental.pallas import tpu as pltpu
from jax.sharding import PartitionSpec as P

KVH = 8
HD = 128
D = 8192
GQ = 8
GCOLS = 1280
CTX = 1024
SUF = 64
CAP = 12
OWN_G = 2
MEAN_LIVE = 8

FIRST_WAY = "ring"
NEXT_WAY = "line"

HALVES = 2
HALF_G = KVH // HALVES
PAD = 16
LOG2E = 1.4426950408889634


ANY = pl.BlockSpec(memory_space=pl.ANY)
SMEM = pl.BlockSpec(memory_space=pltpu.SMEM)
VMEM = pl.BlockSpec(memory_space=pltpu.VMEM)
MIB = 1 << 20


def near(x):
    return pltpu.with_memory_space_constraint(x, pltpu.VMEM)


def far(x):
    return pltpu.with_memory_space_constraint(x, pltpu.HBM)


def room(mib):
    return pltpu.CompilerParams(vmem_limit_bytes=mib * MIB)


def snake(chips):
    return chips <= 8 and chips % 2 == 0


def ring_moves(devices):
    chips = devices // 2
    ring = list(range(chips))
    if snake(chips):
        ring = list(range(0, chips, 2)) + list(range(chips - 1, 0, -2))
    forward = [(2 * ring[k], 2 * ring[(k + 1) % chips]) for k in range(chips)]
    backward = [(2 * ring[k] + 1, 2 * ring[k - 1] + 1) for k in range(chips)]
    return forward + backward, [(i, i ^ 1) for i in range(devices)]


def line_moves(devices):
    line = devices // 4
    index = [(i // 4, i // 2 % 2, i % 2) for i in range(devices)]

    def moves(target):
        return [(i, target(*index[i])) for i in range(devices)]

    step = {d: moves(lambda a, b, c, d=d: (a - d) % line * 4 + b * 2 + c) for d in range(1, line)}
    step["pair"] = moves(lambda a, b, c: a * 4 + (1 - b) * 2 + c)
    step["swap"] = moves(lambda a, b, c: a * 4 + b * 2 + 1 - c)
    return line, step


def line_order(line):
    return [0] + sorted(range(1, line), key=lambda d: (-min(d, line - d), d))


def line_owner(devices, m):
    line = devices // 4
    pair, core, distance = m // (2 * line), m // line % 2, line_order(line)[m % line]
    me = lax.axis_index("wide")
    there = (me // 4 + distance) % line
    return 4 * there + 2 * ((me // 2 + pair) % 2) + (me + core) % 2


def line_gather(block, devices):
    line, step = line_moves(devices)
    order = line_order(line)
    here = [block] + [lax.ppermute(block, "wide", step[d]) for d in order[1:]]
    across = [lax.ppermute(part, "wide", step["pair"]) for part in here]
    bundles = []
    for parts in (here, across):
        bundle = join(parts)
        bundles += [bundle, lax.ppermute(bundle, "wide", step["swap"])]
    return bundles


def line_groups(devices):
    return [[0, 1], [2], [3]]


def ring_groups(devices):
    chips = devices // 2
    middle = (chips - 1) // 2
    return [list(r) for r in (range(middle), range(middle, chips - 1), range(chips - 1, chips))]


def ring_owner(devices, m):
    chips = devices // 2
    bundle, second = m // 2, m % 2
    distance, swapped = (bundle + 1) // 2, bundle > 0 and bundle % 2 == 0
    me = lax.axis_index("wide")
    chip, core = me // 2, me % 2
    at = chip
    if snake(chips):
        at = jnp.where(chip % 2 == 0, chip // 2, chips - 1 - chip // 2)
    sign = (2 * core - 1) * (-1 if swapped else 1)
    there = (at + sign * distance + chips) % chips
    if snake(chips):
        there = jnp.where(there < chips // 2, 2 * there, 2 * (chips - 1 - there) + 1)
    return 2 * there + (core + second + (1 if swapped else 0)) % 2


def join_kernel(*refs):
    rows = refs[0].shape[0]
    for i, part in enumerate(refs[:-1]):
        refs[-1][i * rows : (i + 1) * rows, :] = part[...]


def join(parts):
    rows, columns = parts[0].shape
    return pl.pallas_call(
        join_kernel,
        out_shape=pltpu.VMEM((len(parts) * rows, columns), parts[0].dtype),
        in_specs=[VMEM] * len(parts),
        out_specs=VMEM,
        compiler_params=room(1 if len(parts) <= 4 else 16),
        name="join",
    )(*[near(part) for part in parts])


def ring_gather(block, devices):
    chips = devices // 2
    step, swap = ring_moves(devices)
    other = lax.ppermute(block, "wide", swap)
    bundle = join([block, other])
    bundles = [bundle]
    for distance in range(1, chips // 2 + 1):
        bundle = lax.ppermute(bundle, "wide", step)
        bundles.append(bundle)
        if distance < chips // 2:
            bundles.append(lax.ppermute(bundle, "wide", swap))
    return bundles


GATHERS = {
    "ring": (ring_gather, ring_owner, ring_groups),
    "line": (line_gather, line_owner, line_groups),
}
FIRST_OWNER = GATHERS[FIRST_WAY][1]
NEXT_OWNER = GATHERS[NEXT_WAY][1]


def plan_kernel(
    devices,
    counts,
    owners,
    gain,
    select,
    pack,
    spread,
    scale,
    starts,
    begin,
    size,
    seen,
    table,
):
    live = devices * MEAN_LIVE
    rows = devices * PAD
    blocks = devices * OWN_G

    def clear(i, carry):
        size[i] = 0
        begin[i] = 0
        seen[i // OWN_G] = 0
        return carry

    lax.fori_loop(0, blocks, clear, 0)
    kv_group = lax.axis_index("wide") // (devices // KVH)

    def visit(p, running):
        starts[p] = running
        owner = owners[kv_group, p]
        nth = seen[owner]
        seen[owner] = nth + 1

        @pl.when(nth < OWN_G)
        def _():
            begin[owner * OWN_G + nth] = running
            size[owner * OWN_G + nth] = counts[p]

        return running + counts[p]

    lax.fori_loop(0, devices, visit, jnp.int32(0))
    lane = lax.broadcasted_iota(jnp.int32, (CAP, live), 1)
    row = lax.broadcasted_iota(jnp.int32, (CAP, live), 0)
    for i in range(blocks):
        hit = (lane == begin[i] + row) & (row < size[i])
        table[i * CAP : (i + 1) * CAP, :] = hit.astype(jnp.float32)
    select[...] = table[...].astype(jnp.bfloat16)
    lane_slot = lax.broadcasted_iota(jnp.int32, (1, rows), 1) // PAD
    lane_row = lax.broadcasted_iota(jnp.int32, (1, rows), 1) % PAD
    place = jnp.full((1, rows), -1, jnp.int32)
    width = scale.shape[1]
    source = lax.broadcasted_iota(jnp.int32, (PAD, devices * CAP), 1)
    slot_row = lax.broadcasted_iota(jnp.int32, (PAD, devices * CAP), 0)
    for m in range(devices):
        parent = FIRST_OWNER(devices, m)
        owner = NEXT_OWNER(devices, m)
        place = jnp.where(
            (lane_slot == m) & (lane_row < counts[parent]), starts[parent] + lane_row, place
        )
        hit = (source == parent * CAP + slot_row) & (slot_row < CAP)
        spread[m * PAD : (m + 1) * PAD, :] = hit.astype(jnp.float32).astype(jnp.bfloat16)
        scale[m : m + 1, :] = gain[pl.ds(pl.multiple_of(owner * width, width), width)].reshape(
            1, width
        )
    hit = place == lax.broadcasted_iota(jnp.int32, (live, rows), 0)
    pack[...] = hit.astype(jnp.float32).astype(jnp.bfloat16)


def plan(counts, owners, norm_gain, devices, width):
    live = devices * MEAN_LIVE
    rows = devices * PAD
    blocks = devices * OWN_G
    return pl.pallas_call(
        functools.partial(plan_kernel, devices),
        out_shape=[
            pltpu.VMEM((blocks * CAP, live), jnp.bfloat16),
            pltpu.VMEM((live, rows), jnp.bfloat16),
            pltpu.VMEM((rows, devices * CAP), jnp.bfloat16),
            pltpu.VMEM((devices, width), jnp.float32),
        ],
        in_specs=[SMEM, SMEM, VMEM],
        out_specs=[VMEM] * 4,
        scratch_shapes=[
            pltpu.SMEM((devices,), jnp.int32),
            pltpu.SMEM((blocks,), jnp.int32),
            pltpu.SMEM((blocks,), jnp.int32),
            pltpu.SMEM((devices,), jnp.int32),
            pltpu.VMEM((blocks * CAP, live), jnp.float32),
        ],
        compiler_params=room(2 if devices <= 16 else 16),
        cost_estimate=pl.CostEstimate(flops=1000000, bytes_accessed=1000000, transcendentals=0),
        name="plan",
    )(counts, owners.T, norm_gain)


def attend_rows(query_rows, keys, values, suffix, tall, out_ref, ready):
    rows = CAP * GQ
    pair = 2 * SUF
    own_row = lax.broadcasted_iota(jnp.int32, (rows, pair), 0) // GQ
    own_key = lax.broadcasted_iota(jnp.int32, (rows, pair), 1) // SUF
    mine = [own_row == own_key + 2 * j for j in range(CAP // 2)]
    scale = HD ** (-0.5) * LOG2E
    contract = (((1,), (1,)), ((), ()))
    ready(0)
    for g in range(HALF_G):
        lanes = slice(g * HD, (g + 1) * HD)
        for q in range(GQ):
            col = (g * GQ + q) * HD
            tall[pl.ds(q, CAP, stride=GQ), :] = query_rows[:, col : col + HD].astype(jnp.float32)
        query = tall[...].astype(jnp.bfloat16)
        distant = lax.dot_general(query, keys[:, lanes], contract, preferred_element_type=jnp.float32)
        every = lax.dot_general(
            query,
            suffix[:, 0, :, lanes].reshape(CAP * SUF, HD),
            contract,
            preferred_element_type=jnp.float32,
        )
        nearby = jnp.full((rows, pair), -1e30, jnp.float32)
        for j in range(CAP // 2):
            nearby = jnp.where(mine[j], every[:, j * pair : (j + 1) * pair], nearby)
        top = jnp.maximum(
            jnp.max(distant, axis=1, keepdims=True), jnp.max(nearby, axis=1, keepdims=True)
        )
        distant = jnp.exp2((distant - top) * scale)
        nearby = jnp.exp2((nearby - top) * scale)
        total = jnp.sum(distant, axis=1, keepdims=True) + jnp.sum(nearby, axis=1, keepdims=True)
        if g == 0:
            ready(1)
        mixed = jnp.dot(distant.astype(jnp.bfloat16), values[:, lanes], preferred_element_type=jnp.float32)
        wide = jnp.concatenate(
            [jnp.where(mine[j], nearby, 0.0).astype(jnp.bfloat16) for j in range(CAP // 2)], axis=1
        )
        mixed = mixed + jnp.dot(
            wide,
            suffix[:, 1, :, lanes].reshape(CAP * SUF, HD),
            preferred_element_type=jnp.float32,
        )
        tall[...] = mixed / total
        for q in range(GQ):
            out_ref[g * CAP : (g + 1) * CAP, q * HD : (q + 1) * HD] = tall[
                pl.ds(q, CAP, stride=GQ), :
            ].astype(jnp.bfloat16)


def attend_kernel(q_hbm, kv_hbm, suffix_hbm, *refs):
    outs = refs[:HALVES]
    q, kv, suffix, tall, sems = refs[HALVES:]
    columns = HALF_G * GQ * HD
    lanes = HALF_G * HD
    copies = []
    for half in range(HALVES):
        heads, spots = pl.ds(half * columns, columns), pl.ds(half * lanes, lanes)
        moves = [
            (q_hbm.at[0, :, heads], q.at[half]),
            (kv_hbm.at[0, 0, :, spots], kv.at[half, 0]),
            (suffix_hbm.at[0, :, :, :, spots], suffix.at[half]),
            (kv_hbm.at[0, 1, :, spots], kv.at[half, 1]),
        ]
        copies.append(
            [
                pltpu.make_async_copy(source, target, sems.at[half, i])
                for i, (source, target) in enumerate(moves)
            ]
        )
    for copy in copies[0]:
        copy.start()
    for half in range(HALVES):

        def ready(stage, half=half):
            for copy in copies[half][3:] if stage else copies[half][:3]:
                copy.wait()
            if stage == 0 and half + 1 < HALVES:
                for copy in copies[half + 1]:
                    copy.start()

        attend_rows(
            q.at[half], kv.at[half, 0], kv.at[half, 1], suffix.at[half], tall, outs[half], ready
        )


def attend_cost():
    keys = CTX + CAP * SUF
    return pl.CostEstimate(
        flops=4 * KVH * GQ * CAP * keys * HD,
        bytes_accessed=4 * KVH * keys * HD,
        transcendentals=KVH * GQ * CAP * (CTX + SUF),
    )


def attend(queries, prefix_kv, suffix_kv):
    return pl.pallas_call(
        attend_kernel,
        out_shape=[pltpu.VMEM((HALF_G * CAP, GQ * HD), jnp.bfloat16)] * HALVES,
        in_specs=[ANY] * 3,
        out_specs=[VMEM] * HALVES,
        scratch_shapes=[
            pltpu.VMEM((HALVES, CAP, HALF_G * GQ * HD), jnp.bfloat16),
            pltpu.VMEM((HALVES, 2, CTX, HALF_G * HD), jnp.bfloat16),
            pltpu.VMEM((HALVES, CAP, 2, SUF, HALF_G * HD), jnp.bfloat16),
            pltpu.VMEM((GQ * CAP, HD), jnp.float32),
            pltpu.SemaphoreType.DMA((HALVES, 4)),
        ],
        cost_estimate=attend_cost(),
        compiler_params=room(12),
        name="attend",
    )(far(queries), far(prefix_kv), far(suffix_kv))


def mix_kernel(half, slots, count, *refs):
    pieces = refs[:count]
    refs = refs[count:]
    each = slots // count
    weight, lhs = refs[0], refs[-1]
    refs = refs[1:-1]
    depth = GQ * HD
    total = None
    lhs[...] = jnp.zeros_like(lhs)
    for g in range(HALF_G):
        for m in range(slots):
            row = (m % each * HALF_G + g) * CAP
            lhs[m * PAD : m * PAD + CAP, :] = pieces[m // each][row : row + CAP, :]
        first = (half * HALF_G + g) * depth
        term = jnp.dot(
            lhs[...], weight[first : first + depth, :], preferred_element_type=jnp.float32
        )
        total = term if total is None else total + term
    if half < HALVES - 1:
        refs[0][...] = total
        return
    before, pack, spread, residual = refs[:4]
    outs = refs[4:]
    ordered = jnp.dot(spread[...], residual[...], preferred_element_type=jnp.float32)
    stream = (ordered + (before[...] + total)).astype(jnp.bfloat16)
    packed = jnp.dot(
        pack[...], stream, preferred_element_type=jnp.float32
    ).astype(jnp.bfloat16)
    width = packed.shape[1] // len(outs)
    for i, out in enumerate(outs):
        out[...] = packed[:, i * width : (i + 1) * width]


def mix(half, pieces, out_weight, extra, chunks):
    slots = sum(piece.shape[0] for piece in pieces) // (HALF_G * CAP)
    width = out_weight.shape[1]
    rows = slots * PAD
    last = half == HALVES - 1
    depth = GQ * HD
    if last:
        live = slots * MEAN_LIVE
        out_shape = [pltpu.VMEM((live, width // chunks), jnp.bfloat16)] * chunks
    else:
        out_shape = [pltpu.VMEM((rows, width), jnp.float32)]
    operands = [near(piece) for piece in pieces] + [near(out_weight)]
    operands += list(extra)
    return pl.pallas_call(
        functools.partial(mix_kernel, half, slots, len(pieces)),
        out_shape=out_shape,
        in_specs=[VMEM] * len(operands),
        out_specs=[VMEM] * len(out_shape),
        scratch_shapes=[pltpu.VMEM((rows, depth), jnp.bfloat16)],
        cost_estimate=pl.CostEstimate(
            flops=2 * rows * HALF_G * depth * width,
            bytes_accessed=2 * HALF_G * depth * (width + slots * CAP),
            transcendentals=0,
        ),
        compiler_params=room(8 if slots <= 16 else 32),
        name=f"mix_{half}",
    )(*operands)


def project_kernel(devices, spans, chunks, first, last, *refs):
    parts = refs[: len(spans) * chunks]
    gain, weight = refs[len(spans) * chunks : len(spans) * chunks + 2]
    rest = list(refs[len(spans) * chunks + 2 :])
    width = gain.shape[1]
    piece = width // chunks
    live = devices * MEAN_LIVE
    each = parts[0].shape[0] // live
    if first:
        total = squares = None
    else:
        total, squares = rest[0][...], rest[1][...]
        rest = rest[2:]
    for i, q in enumerate(spans):
        for t in range(each):
            m = each * q + t
            scale = gain[m : m + 1, :]
            owner = NEXT_OWNER(devices, m)
            for c in range(chunks):
                rows = pl.ds(pl.multiple_of(owner * width + c * piece, piece), piece)
                wide = parts[i * chunks + c][t * live : (t + 1) * live, :].astype(jnp.float32)
                for lane in range(0, piece, HD):
                    tile = wide[:, lane : lane + HD]
                    squares = tile * tile if squares is None else squares + tile * tile
                scaled = (wide * scale[:, c * piece : (c + 1) * piece]).astype(jnp.bfloat16)
                term = jnp.dot(scaled, weight[rows, :], preferred_element_type=jnp.float32)
                total = term if total is None else total + term
    if not last:
        rest[0][...] = total
        rest[1][...] = squares
        return
    select, out = rest
    inverse = lax.rsqrt(jnp.sum(squares, axis=1, keepdims=True) / D + 1e-05)
    projected = (total * inverse).astype(jnp.bfloat16)
    out[...] = jnp.dot(select[...], projected, preferred_element_type=jnp.float32).astype(
        jnp.bfloat16
    )


def project(spans, parts, gain, weight, before, select):
    chunks = len(parts) // len(spans)
    live = gain.shape[0] * MEAN_LIVE
    width = gain.shape[1]
    columns = weight.shape[1]
    first = before is None
    last = select is not None
    operands = [near(part) for part in parts] + [near(gain), near(weight)]
    specs = [VMEM] * len(parts) + [VMEM, VMEM]
    if not first:
        operands += [near(x) for x in before]
        specs += [VMEM, VMEM]
    if last:
        operands.append(near(select))
        specs.append(VMEM)
        out_shape = jax.ShapeDtypeStruct((select.shape[0], columns), jnp.bfloat16)
        out_specs = VMEM
    else:
        out_shape = [
            pltpu.VMEM((live, columns), jnp.float32),
            pltpu.VMEM((live, HD), jnp.float32),
        ]
        out_specs = [VMEM, VMEM]
    return pl.pallas_call(
        functools.partial(project_kernel, gain.shape[0], tuple(spans), chunks, first, last),
        out_shape=out_shape,
        in_specs=specs,
        out_specs=out_specs,
        cost_estimate=pl.CostEstimate(
            flops=4 * live * len(spans) * width * columns,
            bytes_accessed=4 * len(spans) * width * (columns + live),
            transcendentals=0,
        ),
        compiler_params=room(4 if live <= 128 else 24),
        name="project_last" if last else "project",
    )(*operands)


def body(
    queries, prefix_kv, suffix_kv, counts, residual, out_weight, norm_gain, qkv_weight, owners
):
    devices = lax.axis_size("wide")
    width = residual.shape[1]
    columns = qkv_weight.shape[1]
    chunks = 1

    out_weight, qkv_weight = near(out_weight), near(qkv_weight)
    first_gather = GATHERS[FIRST_WAY][0]
    next_gather, _, next_groups = GATHERS[NEXT_WAY]
    first, second = attend(queries, prefix_kv, suffix_kv)
    first = first_gather(first, devices)
    second = first_gather(second, devices)
    select, pack, spread, gain = plan(counts, owners, norm_gain, devices, width)
    (before,) = mix(0, first, out_weight, (), chunks)
    extra = (near(before), near(pack), near(spread), near(residual))
    packed = mix(1, second, out_weight, extra, chunks)

    parts = [next_gather(part, devices) for part in packed]
    groups = next_groups(devices)
    carried = None
    for spans in groups:
        blocks = [chunk[q] for q in spans for chunk in parts]
        last = spans is groups[-1]
        carried = project(spans, blocks, gain, qkv_weight, carried, select if last else None)
    outgoing = carried.reshape(devices, OWN_G * CAP, columns)
    incoming = lax.all_to_all(outgoing, "wide", split_axis=0, concat_axis=0, tiled=True)
    return incoming.transpose(1, 0, 2).reshape(1, OWN_G, CAP, KVH, GCOLS)


def solution(mesh):
    placed = (
        P(("groups", "wide"), None, None),
        P(("groups", "wide"), None, None, None),
        P(("groups", "wide"), None, None, None, None),
        P("groups"),
        P("groups", "wide"),
        P(None, "wide"),
        P(),
        P(None, "wide"),
        P(),
    )
    return jax.shard_map(
        body,
        mesh=mesh,
        in_specs=placed,
        out_specs=P(("groups", "wide"), None, None, None, None),
        check_vma=False,
    )
```
